256 devices in a mesh: gx: 16 (over x, y), gy: 16 (over z, core).
Axes of the slice: x: 4, y: 4, z: 8, core: 2. Of those that a mesh axis runs over, the one named last changes fastest.
Arguments:
- positions: float32 [3, 524288], P(None, ('gx', 'gy')), may hold values from -6 to 6
- strengths: float32 [3, 524288], P(None, ('gx', 'gy')), may hold values from -2 to 2
- cores: float32 [524288], P(('gx', 'gy')), may hold values from 0.05 to 0.5
- cell_local: int32 [524288], P(('gx', 'gy')), may hold values from 0 to 1
- cell_centers: float32 [3, 512], P(None, ('gx', 'gy')), may hold values from -6 to 6
- send_blocks: int32 [4096, 4], P(('gx', 'gy')), may hold values from 0 to 15, as said below
- pair_src: int32 [16384, 2], P(('gx', 'gy')), may hold values from 0 to 15, as said below
- counts: int32 [4096], P(('gx', 'gy')), may hold values from 1 to 4
Outputs:
- stretch_first: float32 [3, 524288], P(None, ('gx', 'gy'))
- stretch_second: float32 [3, 524288], P(None, ('gx', 'gy'))
The draws below stay inside these ranges and needn't reach their ends.
Inputs may be any that keep to these rules, and one draw needn't show every extreme that they name: `send_blocks`: each row names 4 different blocks of the sending device. `pair_src`: each row names 2 different blocks of the partner.
All inputs are finite; a program needn't handle non-finite values.
Results may differ from the reference program's by a relative error of at most 0.0003.
Values sent between devices are 32-bit elements; how exact they have to be, the bound alone decides.
A program may use at most 64 MiB of HBM per device.

```python
import math
import jax
import jax.numpy as jnp
from jax import lax

BLOCK = 128
NB = 16
SLOTS = 4
PAIRS = 2
CELLS_DEV = 2
PEERS = 16
NPART = 524288
CELLS = 512
ROUTES = 4096
N_GX = 16
N_GY = 16


def draw_send_blocks(key, part):
    keys = jax.random.split(jax.random.fold_in(key, 11), ROUTES)
    rows = jax.vmap(lambda one_key: jax.random.permutation(one_key, NB)[:SLOTS])(keys)
    return rows.astype(jnp.int32)


def draw_pair_src(key, part):
    keys = jax.random.split(jax.random.fold_in(key, 23), ROUTES * SLOTS)
    rows = jax.vmap(lambda one_key: jax.random.permutation(one_key, NB)[:PAIRS])(keys)
    return rows.astype(jnp.int32)


def draw_counts(key, part):
    drawn = jax.random.randint(jax.random.fold_in(key, 37), (ROUTES,), 1, SLOTS + 1)
    full_route = jnp.arange(ROUTES, dtype=jnp.int32) % PEERS == 0
    return jnp.where(full_route, SLOTS, drawn).astype(jnp.int32)


def with_ends(values, rng, smallest, high):
    shape = values.shape
    index_at = [jax.random.randint(jax.random.fold_in(rng, axis), (), 0, shape[axis]) for axis in range(len(shape))]
    values = values.at[tuple(index_at)].set(smallest)
    longest = shape.index(max(shape))
    index_at[longest] = (index_at[longest] + 1) % shape[longest]
    return values.at[tuple(index_at)].set(high)


def block_levels(own_key, dims, cuts, least, largest):
    loudness, own = 1.0, jax.random.fold_in(own_key, 6)
    for position, shards_of in cuts:
        heights = jnp.exp(jax.random.uniform(jax.random.fold_in(own, position), (shards_of,), jnp.float32, least / len(cuts), largest / len(cuts)))
        loudness = loudness * jnp.repeat(heights, dims[position] // shards_of).reshape([-1 if axis == position else 1 for axis in range(len(dims))])
    return loudness


def centred(rng, dims, width, most, pieces=(), kind=jnp.bfloat16):
    entries = width * jax.random.normal(rng, dims, jnp.float32)
    if pieces:
        entries = entries * block_levels(rng, dims, pieces, -0.22, 0.18)
    return jnp.clip(entries, -most, most).astype(kind)


def setup_inputs(seed: int = 0) -> dict:
    splits = jax.random.split(jax.random.key(seed), 9)
    return {
        "positions": centred(splits[0], (3, NPART), 1.0, 6.0, ((1, 256),), jnp.float32),
        "strengths": centred(splits[1], (3, NPART), 0.3, 2.0, ((1, 256),), jnp.float32),
        "cores": jnp.clip(jnp.exp(math.log(0.5) - 2.3025851 * jax.random.uniform(splits[2], (NPART,), jnp.float32) ** block_levels(splits[2], (NPART,), ((0, 256),), -0.2, 0.2)), 0.05, 0.5),
        "cell_local": with_ends(jax.random.randint(splits[3], (NPART,), 0, CELLS_DEV), jax.random.fold_in(splits[3], 1), 0, CELLS_DEV - 1).astype(jnp.int32),
        "cell_centers": centred(splits[4], (3, CELLS), 1.0, 6.0, ((1, 256),), jnp.float32),
        "send_blocks": draw_send_blocks(jax.random.fold_in(splits[8], 71), 0),
        "pair_src": draw_pair_src(jax.random.fold_in(splits[8], 71), 0),
        "counts": draw_counts(jax.random.fold_in(splits[8], 71), 0),
    }


far_core = 1.0
step_size = 0.1
inv_four_pi = 1.0 / (4.0 * math.pi)

def tile_gradient(tpos, tcore, spos, salpha, score):
    rx = tpos[0][:, None] - spos[0][None, :]
    ry = tpos[1][:, None] - spos[1][None, :]
    rz = tpos[2][:, None] - spos[2][None, :]
    s2 = rx * rx + ry * ry + rz * rz + 0.5 * (tcore[:, None] * tcore[:, None] + score[None, :] * score[None, :])
    inv = lax.rsqrt(s2)
    inv3 = inv * inv * inv
    inv5 = inv3 / s2
    ax = salpha[0][None, :]
    ay = salpha[1][None, :]
    az = salpha[2][None, :]
    w0 = lax.optimization_barrier(jnp.sum(ax * inv3, axis=1))
    w1 = lax.optimization_barrier(jnp.sum(ay * inv3, axis=1))
    w2 = lax.optimization_barrier(jnp.sum(az * inv3, axis=1))
    zero = jnp.zeros_like(w0)
    eps_rows = [[zero, w2, -w1], [-w2, zero, w0], [w1, -w0, zero]]
    crosses = [ry * az - rz * ay, rz * ax - rx * az, rx * ay - ry * ax]
    dists = [rx, ry, rz]
    rows = []
    for first in range(3):
        weighted = crosses[first] * inv5
        for second in range(3):
            term = lax.optimization_barrier(jnp.sum(weighted * dists[second], axis=1))
            rows.append((3.0 * term - eps_rows[first][second]) * inv_four_pi)
    return jnp.stack(rows, axis=0)

def block_gradient(tpos, tcore, sources):
    grads = jax.vmap(lambda source: tile_gradient(tpos, tcore, source[0:3], source[3:6], source[6]))(sources)
    return lax.optimization_barrier(jnp.sum(grads, axis=0))

def stretch_of(alpha, grad):
    rows = []
    for first in range(3):
        rows.append(alpha[..., 0, :] * grad[..., 3 * first, :] + alpha[..., 1, :] * grad[..., 3 * first + 1, :] + alpha[..., 2, :] * grad[..., 3 * first + 2, :])
    return jnp.stack(rows, axis=-2)

def evaluate(positions, alpha, cores, cell_local, cell_centers, send_blocks, pair_src, counts):
    ndev = N_GX * N_GY
    parts = jnp.concatenate([positions, alpha, cores[None, :]], axis=0)
    parts = parts.reshape(7, ndev, NB, BLOCK).transpose(1, 2, 0, 3)
    cell_hot = (cell_local.reshape(ndev, NB, BLOCK)[..., None] == jnp.arange(CELLS_DEV, dtype=jnp.int32)).astype(jnp.float32)
    gamma = jnp.einsum('dtcb,dtbk->cdk', parts[:, :, 3:6, :], cell_hot, precision=lax.Precision.HIGHEST)
    gamma = gamma.reshape(3, CELLS)
    sends = send_blocks.reshape(ndev, PEERS, SLOTS)
    pairs = pair_src.reshape(ndev, PEERS, SLOTS, PAIRS)
    live_counts = counts.reshape(ndev, PEERS)
    far_cores = jnp.full((CELLS,), far_core, dtype=jnp.float32)

    def one_device(device):
        mine = parts[device]
        targets = mine[sends[device]]
        partners = device // PEERS * PEERS + jnp.arange(PEERS, dtype=jnp.int32)
        sources = parts[partners[:, None, None], pairs[device]]
        grads = jax.vmap(jax.vmap(block_gradient))(targets[:, :, 0:3], targets[:, :, 6], sources)
        live = (jnp.arange(SLOTS, dtype=jnp.int32)[None, :] < live_counts[device][:, None]).astype(jnp.float32)
        weight = (sends[device][:, :, None] == jnp.arange(NB, dtype=jnp.int32)[None, None, :]).astype(jnp.float32) * live[:, :, None]
        near = jnp.einsum('gkt,gkcb->tcb', weight, grads, precision=lax.Precision.HIGHEST)
        keep = (jnp.arange(CELLS, dtype=jnp.int32) // CELLS_DEV != device).astype(jnp.float32)
        far_gamma = gamma * keep[None, :]
        far = jax.vmap(lambda target: tile_gradient(target[0:3], target[6], cell_centers, far_gamma, far_cores))(mine)
        stretch = stretch_of(mine[:, 3:6], near + far)
        return stretch.transpose(1, 0, 2).reshape(3, NB * BLOCK)
    result = lax.map(one_device, jnp.arange(ndev, dtype=jnp.int32))
    return result.transpose(1, 0, 2).reshape(3, NPART)

def reference(positions, strengths, cores, cell_local, cell_centers, send_blocks, pair_src, counts):
    stretch_first = evaluate(positions, strengths, cores, cell_local, cell_centers, send_blocks, pair_src, counts)
    moved = strengths + step_size * stretch_first
    stretch_second = evaluate(positions, moved, cores, cell_local, cell_centers, send_blocks, pair_src, counts)
    return (stretch_first, stretch_second)
```

```python
import functools
import math

import jax
import jax.numpy as jnp
from jax import lax
from jax.experimental import pallas as pl
from jax.experimental.pallas import tpu as pltpu
from jax.sharding import PartitionSpec as P

BLOCK = 128
NB = 16
SLOTS = 4
GX_GY = ("gx", "gy")
F32 = jnp.float32
BF16 = jnp.bfloat16

far_core = 1.0
step_size = 0.1
inv_four_pi = 1.0 / (4.0 * math.pi)

PEERS = 16
CHIPS = 8
NEAR = PEERS * SLOTS
UNITS = NEAR + 2 * NB
SRC = PEERS * NB


def dot_t(left, right):
    return lax.dot_general(left, right, (((1,), (1,)), ((), ())), preferred_element_type=F32)


def rounded(value):
    return value.astype(BF16).astype(F32)


def kernel(
    pos, strg, cor, cell, cen, sb, pr, cnt,
    out1, out2,
    land, land2, gxa, gya, gxb, gyb,
    tb, ta, sp, ab, w, pb, k5, rm, rk, nm, nk,
    ring_s, ring_r, ring2_s, ring2_r, gxs, gxr, gys, gyr, gxs2, gxr2, gys2, gyr2,
):
    gx, gy = lax.axis_index("gx"), lax.axis_index("gy")
    z, c = gy // 2, gy % 2
    sgn = 1 - 2 * c

    def chip(offset):
        return (z + offset + CHIPS) % CHIPS

    barrier = pltpu.get_barrier_semaphore()

    @pl.loop(1, PEERS)
    def _(d):
        pl.semaphore_signal(
            barrier, inc=1, device_id={"gx": (gx + d) % PEERS},
            device_id_type=pl.DeviceIdType.MESH)
        pl.semaphore_signal(
            barrier, inc=1, device_id={"gy": (gy + d) % PEERS},
            device_id_type=pl.DeviceIdType.MESH)

    for b in range(NB):
        cols = slice(b * BLOCK, (b + 1) * BLOCK)
        for r in range(3):
            land[gy, r, b : b + 1, :] = pos[r : r + 1, cols]
            land[gy, 3 + r, b : b + 1, :] = strg[r : r + 1, cols]
    land[gy, 6] = 0.5 * cor[...] * cor[...]

    rows8 = lax.broadcasted_iota(jnp.int32, (8, BLOCK), 0)
    lanes8 = lax.broadcasted_iota(jnp.int32, (8, BLOCK), 1)
    my_lane = 32 * (gy % 4) + 2 * gx

    def cell_tile(comps, centers):
        tile = jnp.zeros((8, BLOCK), F32)
        for one in range(2):
            here = lanes8 == my_lane + one
            chosen = (cell[...] == one).astype(F32)
            for r in range(3):
                total = jnp.sum(comps[r] * chosen, axis=(0, 1), keepdims=True)
                tile = jnp.where(here & (rows8 == r), total, tile)
                if centers:
                    tile = jnp.where(here & (rows8 == 3 + r), cen[r, one], tile)
        return tile

    gxa[gx] = cell_tile([land[gy, 3 + r] for r in range(3)], True)

    def remote(src, dst, ss, rs, where):
        return pltpu.make_async_remote_copy(
            src_ref=src, dst_ref=dst, send_sem=ss, recv_sem=rs,
            device_id=where, device_id_type=pl.DeviceIdType.MESH)

    def spread(buf, me, axis, ss, rs):
        @pl.loop(1, PEERS)
        def _(d):
            remote(buf.at[me], buf.at[me], ss.at[d], rs.at[d], {axis: (me + d) % PEERS}).start()

    def spread_recv(buf, me, axis, ss, rs):
        @pl.loop(1, PEERS)
        def _(d):
            of = (me - d + PEERS) % PEERS
            remote(buf.at[of], buf.at[of], ss.at[d], rs.at[d], {axis: (me + d) % PEERS}).wait_recv()

    def spread_sent(buf, me, axis, ss, rs):
        @pl.loop(1, PEERS)
        def _(d):
            remote(buf.at[me], buf.at[me], ss.at[d], rs.at[d], {axis: (me + d) % PEERS}).wait_send()

    sibling = z * 2 + 1 - c

    def ring_a(buf, s, ss, rs):
        owner = chip(-(s - 1) * sgn) * 2 + c
        return remote(buf.at[owner], buf.at[owner], ss.at[s - 1], rs.at[s - 1],
                      {"gy": chip(sgn) * 2 + c})

    def ring_b(buf, s, ss, rs):
        owner = chip((s - 1) * sgn) * 2 + c
        return remote(buf.at[owner], buf.at[owner], ss.at[3 + s], rs.at[3 + s],
                      {"gy": chip(-sgn) * 2 + c})

    def across(buf, j, ss, rs):
        off = 0 if j == 0 else (-j * sgn if j <= 4 else (j - 4) * sgn)
        owner = chip(off) * 2 + c
        return remote(buf.at[owner], buf.at[owner], ss.at[7 + j], rs.at[7 + j], {"gy": sibling})

    def ring_a_recv(buf, s, ss, rs):
        owner = chip(-s * sgn) * 2 + c
        remote(buf.at[owner], buf.at[owner], ss.at[s - 1], rs.at[s - 1],
               {"gy": chip(sgn) * 2 + c}).wait_recv()

    def ring_b_recv(buf, s, ss, rs):
        owner = chip(s * sgn) * 2 + c
        remote(buf.at[owner], buf.at[owner], ss.at[3 + s], rs.at[3 + s],
               {"gy": chip(-sgn) * 2 + c}).wait_recv()

    def across_recv(buf, j, ss, rs):
        off = 0 if j == 0 else (j * sgn if j <= 4 else -(j - 4) * sgn)
        owner = chip(off) * 2 + 1 - c
        remote(buf.at[owner], buf.at[owner], ss.at[7 + j], rs.at[7 + j],
               {"gy": sibling}).wait_recv()

    def ring_start(buf, ss, rs):
        ring_a(buf, 1, ss, rs).start()
        ring_b(buf, 1, ss, rs).start()
        across(buf, 0, ss, rs).start()

    def ring_step(buf, s, ss, rs):
        ring_a_recv(buf, s, ss, rs)
        if s < 4:
            ring_a(buf, s + 1, ss, rs).start()
        across(buf, s, ss, rs).start()
        if s < 4:
            ring_b_recv(buf, s, ss, rs)
            if s < 3:
                ring_b(buf, s + 1, ss, rs).start()
            across(buf, 4 + s, ss, rs).start()

    def ring_sent(buf, ss, rs):
        for s in range(1, 5):
            ring_a(buf, s, ss, rs).wait_send()
            if s < 4:
                ring_b(buf, s, ss, rs).wait_send()
        for j in range(8):
            across(buf, j, ss, rs).wait_send()

    def columns(p, a, base, count):
        b0 = p[1] * a[2] - p[2] * a[1]
        b1 = p[2] * a[0] - p[0] * a[2]
        b2 = p[0] * a[1] - p[1] * a[0]
        for r, value in enumerate([a[0], a[1], a[2], b0, b1, b2]):
            ab[pl.ds(r, count, stride=8), :] = value
        pieces(base, count)

    def pieces(base, count):
        full = ab[0 : count * 8, :]
        hi = rounded(full)
        rest = full - hi
        mid = rounded(rest)
        low = rest - mid
        nothing = jnp.zeros((8, BLOCK), F32)
        for b in range(count):
            part = slice(b * 8, b * 8 + 8)
            both = jnp.concatenate([hi[part], mid[part]], axis=0)
            w[base + b, 0:16, :] = both.astype(BF16)
            w[base + b, 16:32, :] = jnp.concatenate([low[part], nothing], axis=0).astype(BF16)

    def prep(g):
        p = [land[g, r] for r in range(3)]
        for r, value in enumerate(p + [land[g, 6]]):
            ab[pl.ds(r, NB, stride=8), :] = value
        for b in range(NB):
            sp[g * NB + b] = ab[b * 8 : b * 8 + 8, :]
        columns(p, [land[g, 3 + r] for r in range(3)], g * NB, NB)

    def prep_again(g):
        columns([land[g, r] for r in range(3)], [land2[g, r] for r in range(3)], g * NB, NB)

    def source_rows(s):
        return sp[s]

    def halves(value):
        hi = value.astype(BF16)
        return hi, (value - hi.astype(F32)).astype(BF16)

    def tile_first(u, t, s0, s1):
        tiles = [source_rows(s0), source_rows(s1)]
        spread_rows = [
            [jnp.broadcast_to(tile[r : r + 1, :], (16, BLOCK)) for r in range(4)] for tile in tiles
        ]
        for i in range(8):
            rows = pl.ds(i * 16, 16)
            tx, ty, tz, tc = (tb[t, r, rows, :] for r in range(4))
            ax, ay, az = (ta[t, r, rows, :] for r in range(3))
            for h in range(2):
                cols = slice(h * BLOCK, (h + 1) * BLOCK)
                sx, sy, sz, sc = spread_rows[h]
                rx, ry, rz = tx - sx, ty - sy, tz - sz
                q = (rx * rx + ry * ry) + (rz * rz + (tc + sc))
                inv = lax.rsqrt(q)
                inv2 = inv * inv
                k3 = inv2 * inv
                five = k3 * inv2
                k5[u, rows, cols] = five
                m = five * (rx * ax + ry * ay + rz * az)
                for j, piece in enumerate([*halves(m), *halves(k3)]):
                    pb[u, pl.ds(j * BLOCK + i * 16, 16), cols] = piece

    def tile_second(u, t, s0, s1):
        tiles = [source_rows(s0), source_rows(s1)]
        spread_rows = [
            [jnp.broadcast_to(tile[r : r + 1, :], (16, BLOCK)) for r in range(3)] for tile in tiles
        ]
        for i in range(8):
            rows = pl.ds(i * 16, 16)
            tx, ty, tz = (tb[t, r, rows, :] for r in range(3))
            ax, ay, az = (ta[t, r, rows, :] for r in range(3))
            for h in range(2):
                cols = slice(h * BLOCK, (h + 1) * BLOCK)
                sx, sy, sz = spread_rows[h]
                rx, ry, rz = tx - sx, ty - sy, tz - sz
                m = k5[u, rows, cols] * (rx * ax + ry * ay + rz * az)
                for j, piece in enumerate(halves(m)):
                    pb[u, pl.ds(j * BLOCK + i * 16, 16), cols] = piece

    def source_columns(s):
        return w[s]

    def near_products(u):
        g = u // SLOTS
        products(u, g * NB + pr[u, 0], g * NB + pr[u, 1])

    def far_products(u):
        half = u % 2
        products(u, SRC + 2 * half, SRC + 2 * half + 1)

    def products(u, s0, s1):
        left = jnp.concatenate([source_columns(s0), source_columns(s1)], axis=1)
        got = dot_t(left, pb[u])

        def folded(first):
            part = got[:, first : first + BLOCK] + got[:, first + BLOCK : first + 2 * BLOCK]
            return part[0:8] + part[8:16] + part[16:24]

        rm[u] = folded(0)
        rk[u] = folded(2 * BLOCK)

    def near_unit(g, k):
        u = g * SLOTS + k
        return u, sb[g, k], g * NB + pr[u, 0], g * NB + pr[u, 1]

    def far_unit(index):
        t, half = index // 2, index % 2
        return NEAR + index, t, SRC + 2 * half, SRC + 2 * half + 1

    def first_pass(unit_of, count, before, finish_one=near_products):
        def body(index, carry):
            finish_one(carry)
            u, t, s0, s1 = unit_of(index)
            tile_first(u, t, s0, s1)
            return u

        return lax.fori_loop(0, count, body, before)

    def near_units(owner_of):
        return lambda index: near_unit(owner_of(index // SLOTS), index % SLOTS)

    def prep_all(owner_of, count, how):
        @pl.loop(0, count)
        def _(j):
            how(owner_of(j))

    def mine_at(s):
        return lambda j: chip((2 * j - 1) * s * sgn) * 2 + c

    def theirs_at(s):
        return lambda j: chip((1 - 2 * j) * s * sgn) * 2 + 1 - c

    def far_rows(buf):
        tiles = []
        for four in range(4):
            total = buf[4 * four]
            for one in range(1, 4):
                total = total + buf[4 * four + one]
            own = (four == gy // 4) & ((lanes8 == my_lane) | (lanes8 == my_lane + 1))
            tiles.append(jnp.where(own & (rows8 < 3), 0.0, total))
        return tiles

    def summed(buf):
        total = buf[0]
        for one in range(1, PEERS):
            total = total + buf[one]
        return total

    def far_columns(tiles, centers):
        for four, tile in enumerate(tiles):
            p = [centers[four][3 + r : 4 + r, :] for r in range(3)]
            a = [tile[r : r + 1, :] for r in range(3)]
            b0 = p[1] * a[2] - p[2] * a[1]
            b1 = p[2] * a[0] - p[0] * a[2]
            b2 = p[0] * a[1] - p[1] * a[0]
            for r, value in enumerate([a[0], a[1], a[2], b0, b1, b2]):
                ab[four * 8 + r : four * 8 + r + 1, :] = value
        pieces(SRC, 4)

    def broadcast_targets(ref, rows_of):
        @pl.loop(0, NB)
        def _(t):
            for r, row in enumerate(rows_of):
                line = row(t)
                ref[t, r] = jnp.broadcast_to(line, (BLOCK, BLOCK)).T

    def land_row(r):
        return lambda t: land[gy, r, pl.ds(t, 1), :]

    broadcast_targets(tb, [land_row(r) for r in (0, 1, 2, 6)])
    broadcast_targets(ta, [land_row(r) for r in (3, 4, 5)])
    ab[...] = jnp.zeros_like(ab)

    lane_u = lax.broadcasted_iota(jnp.int32, (8, UNITS * 8), 1)
    unit_u = lane_u // 8
    row_u = lax.broadcasted_iota(jnp.int32, (8, UNITS * 8), 0)
    fed = jnp.where(unit_u >= NEAR, (unit_u - NEAR) // 2, -1)
    live = jnp.ones_like(fed)
    for g in range(PEERS):
        for k in range(SLOTS):
            here = unit_u == g * SLOTS + k
            fed = jnp.where(here, sb[g, k], fed)
            live = jnp.where(here, cnt[g] - k, live)
    same = (lane_u % 8 == row_u) & (live > 0)
    select = jnp.concatenate(
        [jnp.where(same & (fed == t), 1.0, 0.0).astype(F32) for t in range(NB)], axis=0
    ).astype(BF16)

    pl.semaphore_wait(barrier, 2 * (PEERS - 1))

    ring_start(land, ring_s, ring_r)
    spread(gxa, gx, "gx", gxs, gxr)

    prep(gy)
    u, t, s0, s1 = near_unit(gy, 0)
    tile_first(u, t, s0, s1)
    carry = u
    carry = first_pass(lambda index: near_unit(gy, index + 1), 3, carry)

    spread_recv(gxa, gx, "gx", gxs, gxr)
    gya[gy] = summed(gxa)
    spread(gya, gy, "gy", gys, gyr)

    across_recv(land, 0, ring_s, ring_r)
    prep(sibling)
    carry = first_pass(lambda index: near_unit(sibling, index), SLOTS, carry)
    for s in range(1, 5):
        ring_step(land, s, ring_s, ring_r)
        count = 2 if s < 4 else 1
        prep_all(mine_at(s), count, prep)
        carry = first_pass(near_units(mine_at(s)), count * SLOTS, carry)
        across_recv(land, s, ring_s, ring_r)
        if s < 4:
            across_recv(land, 4 + s, ring_s, ring_r)
        prep_all(theirs_at(s), count, prep)
        carry = first_pass(near_units(theirs_at(s)), count * SLOTS, carry)

    spread_recv(gya, gy, "gy", gys, gyr)
    centers = far_rows(gya)
    for four in range(4):
        for r in range(3):
            sp[SRC + four, r : r + 1, :] = centers[four][3 + r : 4 + r, :]
        sp[SRC + four, 3:4, :] = jnp.full((1, BLOCK), 0.5 * far_core * far_core, F32)
    far_columns(centers, centers)
    near_products(carry)
    u, t, s0, s1 = far_unit(0)
    tile_first(u, t, s0, s1)
    carry = first_pass(lambda index: far_unit(index + 1), 2 * NB - 1, u, far_products)
    far_products(carry)

    def finish(a, p, out):
        for many, one in ((rm, nm), (rk, nk)):
            full = many[...].reshape(UNITS * 8, BLOCK)
            hi = full.astype(BF16)
            rest = full - hi.astype(F32)
            mid = rest.astype(BF16)
            low = (rest - mid.astype(F32)).astype(BF16)
            one[...] = (
                jnp.dot(select, hi, preferred_element_type=F32)
                + jnp.dot(select, mid, preferred_element_type=F32)
                + jnp.dot(select, low, preferred_element_type=F32)
            )
        sa = [nm[pl.ds(r, NB, stride=8), :] for r in range(3)]
        sq = [nm[pl.ds(3 + r, NB, stride=8), :] for r in range(3)]
        sk = [nk[pl.ds(r, NB, stride=8), :] for r in range(3)]
        result = []
        for r in range(3):
            i, j = (r + 1) % 3, (r + 2) % 3
            turned = p[i] * sa[j] - p[j] * sa[i] - sq[r]
            twisted = a[i] * sk[j] - a[j] * sk[i]
            result.append((3.0 * turned - twisted) * inv_four_pi)
        for r in range(3):
            for b in range(NB):
                out[r : r + 1, b * BLOCK : (b + 1) * BLOCK] = result[r][b : b + 1, :]
        return result

    first = finish([land[gy, 3 + r] for r in range(3)], [land[gy, r] for r in range(3)], out1)

    for r in range(3):
        land2[gy, r] = land[gy, 3 + r] + step_size * first[r]
    moved = [land2[gy, r] for r in range(3)]
    gxb[gx] = cell_tile(moved, False)
    spread(gxb, gx, "gx", gxs2, gxr2)
    ring_start(land2, ring2_s, ring2_r)

    broadcast_targets(ta, [(lambda t, r=r: land2[gy, r, pl.ds(t, 1), :]) for r in range(3)])
    spread_recv(gxb, gx, "gx", gxs2, gxr2)
    gyb[gy] = summed(gxb)
    spread(gyb, gy, "gy", gys2, gyr2)

    def second_tiles(unit_of, first_index, last_index):
        @pl.loop(first_index, last_index)
        def _(index):
            tile_second(*unit_of(index))

    by_slot = lambda index: near_unit(index // SLOTS, index % SLOTS)
    for s in range(1, 5):
        second_tiles(by_slot, (s - 1) * 16, s * 16)
        ring_step(land2, s, ring2_s, ring2_r)
    second_tiles(far_unit, 0, 2 * NB)

    def second_products(g):
        prep_again(g)
        for k in range(SLOTS):
            u, t, s0, s1 = near_unit(g, k)
            products(u, s0, s1)

    for j in range(8):
        across_recv(land2, j, ring2_s, ring2_r)

    @pl.loop(0, PEERS)
    def _(g):
        second_products(g)

    spread_recv(gyb, gy, "gy", gys2, gyr2)
    far_columns(far_rows(gyb), centers)

    @pl.loop(0, NB // 2)
    def _(index):
        for one in range(4):
            u, t, s0, s1 = far_unit(index * 4 + one)
            products(u, s0, s1)

    finish(moved, [land[gy, r] for r in range(3)], out2)

    ring_sent(land, ring_s, ring_r)
    ring_sent(land2, ring2_s, ring2_r)
    spread_sent(gxa, gx, "gx", gxs, gxr)
    spread_sent(gya, gy, "gy", gys, gyr)
    spread_sent(gxb, gx, "gx", gxs2, gxr2)
    spread_sent(gyb, gy, "gy", gys2, gyr2)


def body(positions, strengths, cores, cell_local, cell_centers, send_blocks, pair_src, counts):
    vmem = pl.BlockSpec(memory_space=pltpu.VMEM)
    smem = pl.BlockSpec(memory_space=pltpu.SMEM)
    dma = pltpu.SemaphoreType.DMA
    shape = jax.ShapeDtypeStruct(positions.shape, F32)
    return pl.pallas_call(
        kernel,
        out_shape=(shape, shape),
        in_specs=[vmem] * 4 + [smem] * 4,
        out_specs=(vmem, vmem),
        scratch_shapes=[
            pltpu.VMEM((PEERS, 7, NB, BLOCK), F32),
            pltpu.VMEM((PEERS, 3, NB, BLOCK), F32),
            pltpu.VMEM((PEERS, 8, BLOCK), F32),
            pltpu.VMEM((PEERS, 8, BLOCK), F32),
            pltpu.VMEM((PEERS, 8, BLOCK), F32),
            pltpu.VMEM((PEERS, 8, BLOCK), F32),
            pltpu.VMEM((NB, 4, BLOCK, BLOCK), F32),
            pltpu.VMEM((NB, 3, BLOCK, BLOCK), F32),
            pltpu.VMEM((SRC + 4, 8, BLOCK), F32),
            pltpu.VMEM((NB * 8, BLOCK), F32),
            pltpu.VMEM((SRC + 4, 32, BLOCK), BF16),
            pltpu.VMEM((UNITS, 4 * BLOCK, 2 * BLOCK), BF16),
            pltpu.VMEM((UNITS, BLOCK, 2 * BLOCK), F32),
            pltpu.VMEM((UNITS, 8, BLOCK), F32),
            pltpu.VMEM((UNITS, 8, BLOCK), F32),
            pltpu.VMEM((NB * 8, BLOCK), F32),
            pltpu.VMEM((NB * 8, BLOCK), F32),
            dma((15,)), dma((15,)), dma((15,)), dma((15,)),
            dma((PEERS,)), dma((PEERS,)), dma((PEERS,)), dma((PEERS,)),
            dma((PEERS,)), dma((PEERS,)), dma((PEERS,)), dma((PEERS,)),
        ],
        compiler_params=pltpu.CompilerParams(
            collective_id=0, has_side_effects=True, vmem_limit_bytes=62 << 20),
        name="vortex",
    )(positions, strengths, cores.reshape(NB, BLOCK), cell_local.reshape(NB, BLOCK),
      cell_centers, send_blocks, pair_src, counts)


def solution(mesh):
    placed = (
        P(None, GX_GY), P(None, GX_GY), P(GX_GY), P(GX_GY),
        P(None, GX_GY), P(GX_GY, None), P(GX_GY, None), P(GX_GY),
    )
    return jax.shard_map(
        body, mesh=mesh, in_specs=placed,
        out_specs=(P(None, GX_GY), P(None, GX_GY)), check_vma=False)
```
